128 devices in a mesh: layer: 4 (over z), panel: 32 (over x, y, core).
Axes of the slice: x: 4, y: 4, z: 4, core: 2. Of those that a mesh axis runs over, the one named last changes fastest.
Arguments:
- reflections: float32 [32, 1024, 1024], P(None, 'panel'), may hold values from -0.95 to 0.95
- wave_decay: float32 [32, 1024], replicated, may hold values from 0.3 to 3
- thickness: float32 [4], P('layer'), may hold values from 0.4 to 1
- material: int32 [4], P('layer'), may hold values from 0 to 31
Outputs:
- stack_blocks: float32 [4, 1024, 1024], P('layer', 'panel')
The draws below stay inside these ranges and needn't reach their ends.
All inputs are finite; a program needn't handle non-finite values.
Results may differ from the reference program's by a relative error of at most 0.00014.
Values sent between devices are 32-bit elements; how exact they have to be, the bound alone decides.
No kernel may reach another device: no remote copies, remote signals or barrier semaphores. Data moves between devices by JAX's collectives and lax.ppermute only.
A program may use at most 128 MiB of HBM per device.

```python
import math
import jax
import jax.numpy as jnp
from jax import lax

ORDER = 1024
MATERIALS = 32
TERMS = 6
LAYERS = 4


def draw_reflections(key, part):
    key_mag = jax.random.fold_in(key, 11)
    key_sign = jax.random.fold_in(key, 12)
    key_off = jax.random.fold_in(key, 13)
    shape = (MATERIALS, ORDER, ORDER)
    diag_mag = jax.random.uniform(key_mag, (MATERIALS, ORDER), jnp.float32, 0.6, 0.9)
    signs = jnp.where(jax.random.bernoulli(key_sign, 0.5, (MATERIALS, ORDER)), 1.0, -1.0)
    spread = 0.16 / math.sqrt(ORDER)
    off_part = jax.random.truncated_normal(key_off, -4.0, 4.0, shape, jnp.float32) * spread
    row_ids = lax_rows(shape)
    col_ids = lax_cols(shape)
    identity = jnp.where(row_ids == col_ids, 1.0, 0.0).astype(jnp.float32)
    return off_part * (1.0 - identity) + identity * (diag_mag * signs)[:, :, None]


def lax_rows(shape):
    return jnp.broadcast_to(jnp.arange(shape[1], dtype=jnp.int32)[None, :, None], shape)


def lax_cols(shape):
    return jnp.broadcast_to(jnp.arange(shape[2], dtype=jnp.int32)[None, None, :], shape)


def plant(values, key, smallest, top_value):
    longest = values.shape.index(max(values.shape))
    spots = []
    for shift in (0, 1):
        where = [jax.random.randint(jax.random.fold_in(key, axis), (), 0, length) for axis, length in enumerate(values.shape)]
        where[longest] = (where[longest] + shift) % values.shape[longest]
        spots.append(tuple(where))
    return values.at[spots[0]].set(smallest).at[spots[1]].set(top_value)


def level_of(own_key, shape, shards, low, top_value):
    loudness, own = 1.0, jax.random.fold_in(own_key, 6)
    for position, shards_of in shards:
        draws = jnp.exp(jax.random.uniform(jax.random.fold_in(own, position), (shards_of,), jnp.float32, low / len(shards), top_value / len(shards)))
        loudness = loudness * jnp.repeat(draws, shape[position] // shards_of).reshape([-1 if axis == position else 1 for axis in range(len(shape))])
    return loudness


def setup_inputs(seed: int = 0) -> dict:
    splits = jax.random.split(jax.random.key(seed), 5)
    return {
        "reflections": draw_reflections(jax.random.fold_in(splits[4], 71), 0),
        "wave_decay": jnp.clip(jnp.exp(jax.random.uniform(splits[1], (MATERIALS, ORDER), jnp.float32, math.log(0.3), math.log(3.0))), 0.3, 3.0),
        "thickness": jnp.clip(0.4 + 0.6 * jax.random.uniform(splits[2], (LAYERS,), jnp.float32) ** level_of(splits[2], (LAYERS,), ((0, 4),), -0.2, 0.2), 0.4, 1.0),
        "material": plant(jax.random.randint(splits[3], (LAYERS,), 0, MATERIALS), jax.random.fold_in(splits[3], 1), 0, MATERIALS - 1).astype(jnp.int32),
    }


def product(left_side, right_side):
    return jnp.dot(left_side, right_side, precision=lax.Precision.HIGHEST, preferred_element_type=jnp.float32)


def series_sum(start_rows, factor_one, factor_two):
    term_now = start_rows
    summed = start_rows
    for _ in range(TERMS - 1):
        term_now = product(product(term_now, factor_one), factor_two)
        summed = summed + term_now
    return summed


def build_layer(refl_full, decays):
    identity = jnp.eye(refl_full.shape[0], dtype=jnp.float32)
    scaled_refl = decays[:, None] * refl_full
    summed = series_sum(identity, scaled_refl, scaled_refl)
    numer = decays[:, None] * refl_full * decays[None, :] - refl_full
    reflect_block = product(summed, numer)
    scaled_sum = summed * decays[None, :]
    trans_block = scaled_sum - product(product(scaled_sum, refl_full), refl_full)
    return (reflect_block, trans_block, trans_block, reflect_block)


def star_product(front_part, back_part):
    upper_chain = series_sum(front_part[1], back_part[0], front_part[3])
    lower_chain = series_sum(back_part[2], front_part[3], back_part[0])
    block_one = front_part[0] + product(product(upper_chain, back_part[0]), front_part[2])
    block_two = product(upper_chain, back_part[1])
    block_three = product(lower_chain, front_part[2])
    block_four = back_part[3] + product(product(lower_chain, front_part[3]), back_part[1])
    return (block_one, block_two, block_three, block_four)


def reference(reflections, wave_decay, thickness, material):
    stacks = []
    for layer_index in range(LAYERS):
        chosen = material[layer_index].astype(jnp.int32)
        refl_full = lax.dynamic_index_in_dim(reflections, chosen, 0, keepdims=False)
        decays = jnp.exp(-lax.dynamic_index_in_dim(wave_decay, chosen, 0, keepdims=False) * thickness[layer_index])
        stacks.append(build_layer(refl_full, decays))
    while len(stacks) > 1:
        stacks = [star_product(stacks[2 * pair], stacks[2 * pair + 1]) for pair in range(len(stacks) // 2)]
    return jnp.stack(stacks[0])
```

```python
import jax
import jax.numpy as jnp
from jax import lax
from jax.experimental import pallas as pl
from jax.experimental.pallas import tpu as pltpu
from jax.sharding import PartitionSpec as P

TERMS = 6
CHUNKS = 8
VMEM_BYTES = 56 * 1024 * 1024


def halves(value):
    high = value.astype(jnp.bfloat16)
    low = (value - high.astype(jnp.float32)).astype(jnp.bfloat16)
    return high, low


def product(rows, high_ref, low_ref):
    count = rows.shape[0]
    high, low = halves(rows)
    both = jnp.concatenate([high, low], axis=0)
    by_high = jnp.dot(both, high_ref[...], preferred_element_type=jnp.float32)
    by_low = jnp.dot(high, low_ref[...], preferred_element_type=jnp.float32)
    return by_high[:count] + (by_high[count:] + by_low)


def fetch(source, slot, stage, sems):
    per_chunk = source.shape[0] // CHUNKS
    for c in range(CHUNKS):
        part = pl.ds(c * per_chunk, per_chunk)
        pltpu.make_async_copy(source.at[part, slot], stage.at[part], sems.at[c]).start()


def split(source, slot, stage, sems, high_ref, low_ref):
    panels, panel_rows, order = stage.shape
    per_chunk = panels // CHUNKS
    chunk_rows = per_chunk * panel_rows

    def body(c, carry):
        part = pl.ds(c * per_chunk, per_chunk)
        pltpu.make_async_copy(source.at[part, slot], stage.at[part], sems.at[c]).wait()
        high, low = halves(stage[part].reshape(chunk_rows, order))
        rows = pl.ds(pl.multiple_of(c * chunk_rows, chunk_rows), chunk_rows)
        high_ref[rows, :] = high
        low_ref[rows, :] = low
        return carry

    lax.fori_loop(0, CHUNKS, body, 0)


def layer_kernel(full, own, decay_row, decay_col, eye, refl_out, trans_out, stage, high, low, sems):
    fetch(full, 0, stage, sems)
    split(full, 0, stage, sems, high, low)
    decays = decay_row[...]
    term = product(decay_col[...] * own[...] * decays, high, low)

    def body(k, carry):
        term, summed = carry
        term = product(term * decays, high, low)
        term = product(term * decays, high, low)
        return term, summed + term

    _, summed = lax.fori_loop(0, TERMS - 2, body, (term, eye[...] + term))
    count = summed.shape[0]
    scaled = summed * decays
    both = product(jnp.concatenate([scaled, summed], axis=0), high, low)
    refl_out[...] = both[:count] * decays - both[count:]
    trans_out[...] = scaled - product(both[:count], high, low)


def pair_kernel(full, start_own, start_oth, own_refl, refl_out, trans_out, stage, high, low, sems):
    for slot in (1, 0, 2):
        fetch(full, slot, stage.at[slot], sems.at[slot])
    split(full, 1, stage.at[1], sems.at[1], high.at[1], low.at[1])
    split(full, 0, stage.at[0], sems.at[0], high.at[0], low.at[0])
    split(full, 2, stage.at[2], sems.at[2], high.at[2], low.at[2])
    count = start_own.shape[0]
    first = product(start_own[...], high.at[1], low.at[1])
    both = jnp.concatenate([first, start_oth[...]], axis=0)

    def body(k, carry):
        both, summed = carry
        both = product(both, high.at[0], low.at[0])
        both = product(both, high.at[1], low.at[1])
        return both, summed + both

    _, summed = lax.fori_loop(0, TERMS - 1, body, (both, both))
    done = product(summed, high.at[2], low.at[2])
    refl_out[...] = own_refl[...] + done[:count]
    trans_out[...] = done[count:]


def last_kernel(full, start, base, weights, out, stage, high, low, sems):
    for slot in (0, 1, 2):
        fetch(full, slot, stage.at[slot], sems.at[slot])
    for slot in (0, 1, 2):
        split(full, slot, stage.at[slot], sems.at[slot], high.at[slot], low.at[slot])
    term = start[...]
    half = product(term, high.at[0], low.at[0])

    def body(k, carry):
        half, term_sum, half_sum = carry
        term = product(half, high.at[1], low.at[1])
        half = product(term, high.at[0], low.at[0])
        return half, term_sum + term, half_sum + half

    _, term_sum, half_sum = lax.fori_loop(0, TERMS - 1, body, (half, term, half))
    chosen = jnp.where(weights[...] > 0.0, half_sum, term_sum)
    out[...] = base[...] + product(chosen, high.at[2], low.at[2])


def call(kernel, slots, outs, panels, panel_rows, order, full, *small):
    lead = (slots,) if slots > 1 else ()
    rows = jax.ShapeDtypeStruct((panel_rows, order), jnp.float32)
    return pl.pallas_call(
        kernel,
        out_shape=(rows,) * outs if outs > 1 else rows,
        in_specs=[pl.BlockSpec(memory_space=pl.ANY)]
        + [pl.BlockSpec(memory_space=pltpu.VMEM)] * len(small),
        out_specs=(pl.BlockSpec(memory_space=pltpu.VMEM),) * outs
        if outs > 1
        else pl.BlockSpec(memory_space=pltpu.VMEM),
        scratch_shapes=[
            pltpu.VMEM(lead + (panels, panel_rows, order), jnp.float32),
            pltpu.VMEM(lead + (order, order), jnp.bfloat16),
            pltpu.VMEM(lead + (order, order), jnp.bfloat16),
            pltpu.SemaphoreType.DMA(lead + (CHUNKS,)),
        ],
        compiler_params=pltpu.CompilerParams(vmem_limit_bytes=VMEM_BYTES),
    )(full, *small)


def gathered(*rows):
    return lax.all_gather(jnp.stack(rows), "panel", axis=0, tiled=False)


def local(reflections, wave_decay, thickness, material):
    panel_rows = reflections.shape[1]
    order = reflections.shape[2]
    panels = order // panel_rows
    sizes = (panels, panel_rows, order)
    row_start = lax.axis_index("panel") * panel_rows
    layer = lax.axis_index("layer")
    chosen = material[0]
    refl_rows = lax.dynamic_index_in_dim(reflections, chosen, 0, keepdims=False)
    decays = jnp.exp(
        -lax.dynamic_index_in_dim(wave_decay, chosen, 0, keepdims=False) * thickness[0]
    )
    own_decays = lax.dynamic_slice_in_dim(decays, row_start, panel_rows)
    row_ids = row_start + jnp.arange(panel_rows, dtype=jnp.int32)
    eye = jnp.where(
        row_ids[:, None] == jnp.arange(order, dtype=jnp.int32)[None, :], 1.0, 0.0
    ).astype(jnp.float32)
    refl, trans = call(
        layer_kernel, 1, 2, *sizes, gathered(refl_rows), refl_rows, decays[None, :], own_decays[:, None], eye
    )
    oth = lax.ppermute(jnp.stack([refl, trans]), "layer", [(0, 1), (1, 0), (2, 3), (3, 2)])
    refl, trans = call(
        pair_kernel, 3, 2, *sizes, gathered(refl, oth[0], trans), trans, oth[1], refl
    )
    inner = (layer == 1) | (layer == 2)
    near = lax.ppermute(jnp.stack([refl, trans]), "layer", [(1, 0), (2, 3)])
    cross = lax.ppermute(refl, "layer", [(1, 2), (2, 1)])
    far = lax.ppermute(jnp.where(inner, refl, trans), "layer", [(0, 2), (2, 0), (1, 3), (3, 1)])
    first = jnp.where(inner, cross, far)
    second = jnp.where(inner, refl, near[0])
    closing = jnp.where(inner, far, trans)
    start = jnp.where(inner, trans, near[1])
    base = jnp.where(inner, 0.0, refl)
    pick = jnp.full((1, order), jnp.where(inner, 0.0, 1.0), jnp.float32)
    out = call(last_kernel, 3, 1, *sizes, gathered(first, second, closing), start, base, pick)
    return out[None]


def solution(mesh):
    placed = (P(None, "panel", None), P(), P("layer"), P("layer"))
    return jax.shard_map(
        local, mesh=mesh, in_specs=placed, out_specs=P("layer", "panel", None), check_vma=False
    )
```

```python
import jax
import jax.numpy as jnp
from jax import lax
from jax.experimental import pallas as pl
from jax.experimental.pallas import tpu as pltpu
from jax.sharding import PartitionSpec as P

TERMS = 6
SIDE = 4
STEPS = (1, 3, 2)
PIECES = 2 * SIDE
MATRIX_BYTES = 4 * 1024 * 1024


def halves(value):
    high = value.astype(jnp.bfloat16)
    low = (value - high.astype(jnp.float32)).astype(jnp.bfloat16)
    return high, low


def product(rows, high_ref, low_ref):
    count = rows.shape[0]
    high, low = halves(rows)
    both = jnp.concatenate([high, low], axis=0)
    by_high = jnp.dot(both, high_ref[...], preferred_element_type=jnp.float32)
    by_low = jnp.dot(high, low_ref[...], preferred_element_type=jnp.float32)
    return by_high[:count] + (by_high[count:] + by_low)


def split(pieces, places, high_ref, low_ref):
    lines, slots, panel_rows, _ = pieces[0].shape
    for i, piece in enumerate(pieces):

        def body(j, carry, i=i, piece=piece):
            rows = pl.ds(pl.multiple_of(places[i * lines + j] * panel_rows, panel_rows), panel_rows)
            for slot in range(slots):
                high, low = halves(piece[j, slot])
                high_ref[slot, rows, :] = high
                low_ref[slot, rows, :] = low
            return carry

        lax.fori_loop(0, lines, body, 0)


def layer_kernel(*refs):
    pieces, refs = refs[:PIECES], refs[PIECES:]
    places, facts, thickness, own, wave_decay, refl_out, trans_out, high, low = refs
    split(pieces, places, high, low)
    rows, order = own.shape
    decays = jnp.exp(-wave_decay[pl.ds(facts[1], 1), :] * thickness[0])
    row_ids = facts[0] + lax.broadcasted_iota(jnp.int32, (rows, order), 0)
    eye = row_ids == lax.broadcasted_iota(jnp.int32, (rows, order), 1)
    own_decays = jnp.sum(jnp.where(eye, decays, 0.0), axis=1, keepdims=True)
    term = product(own_decays * own[...] * decays, high.at[0], low.at[0])

    def body(k, carry):
        term, summed = carry
        term = product(term * decays, high.at[0], low.at[0])
        term = product(term * decays, high.at[0], low.at[0])
        return term, summed + term

    _, summed = lax.fori_loop(0, TERMS - 2, body, (term, jnp.where(eye, 1.0, 0.0) + term))
    scaled = summed * decays
    both = product(jnp.concatenate([scaled, summed], axis=0), high.at[0], low.at[0])
    refl_out[...] = both[:rows] * decays - both[rows:]
    trans_out[...] = scaled - product(both[:rows], high.at[0], low.at[0])


def pair_chain(*refs):
    pieces, refs = refs[:PIECES], refs[PIECES:]
    places, start_own, start_oth, out, high, low = refs
    split(pieces, places, high, low)
    first = product(start_own[...], high.at[1], low.at[1])
    both = jnp.concatenate([first, start_oth[...]], axis=0)

    def body(k, carry):
        both, summed = carry
        both = product(both, high.at[0], low.at[0])
        both = product(both, high.at[1], low.at[1])
        return both, summed + both

    _, out[...] = lax.fori_loop(0, TERMS - 1, body, (both, both))


def pair_close(*refs):
    pieces, refs = refs[:PIECES], refs[PIECES:]
    places, inner, summed, own_refl, refl_out, trans_out, far_out, high, low = refs
    split(pieces, places, high, low)
    rows = own_refl.shape[0]
    done = product(summed[...], high.at[0], low.at[0])
    refl, trans = own_refl[...] + done[:rows], done[rows:]
    refl_out[...] = refl
    trans_out[...] = trans
    far_out[...] = jnp.where(inner[0] == 1, refl, trans)


def last_chain(*refs):
    pieces, refs = refs[:PIECES], refs[PIECES:]
    places, inner, start, out, high, low = refs
    split(pieces, places, high, low)
    first, second = 1 - inner[0], inner[0]
    term = start[...]
    half = product(term, high.at[first], low.at[first])

    def body(k, carry):
        half, term_sum, half_sum = carry
        term = product(half, high.at[second], low.at[second])
        half = product(term, high.at[first], low.at[first])
        return half, term_sum + term, half_sum + half

    _, term_sum, half_sum = lax.fori_loop(0, TERMS - 1, body, (half, term, half))
    out[...] = jnp.where(inner[0] == 1, term_sum, half_sum)


def last_close(*refs):
    pieces, refs = refs[:PIECES], refs[PIECES:]
    places, inner, summed, own_refl, out, high, low = refs
    split(pieces, places, high, low)
    base = jnp.where(inner[0] == 1, 0.0, own_refl[...])
    out[...] = base + product(summed[...], high.at[0], low.at[0])


def call(kernel, steps, outs, pieces, tables, small, placed=True):
    lines, slots, _, order = pieces[0].shape
    vmem = pl.BlockSpec(memory_space=pltpu.VMEM)
    here = [pltpu.with_memory_space_constraint(a, pltpu.VMEM) for a in (*pieces, *small)]
    out_shape = tuple(
        pltpu.VMEM(shape, jnp.float32) if placed else jax.ShapeDtypeStruct(shape, jnp.float32) for shape in outs
    )
    return pl.pallas_call(
        kernel,
        out_shape=out_shape,
        in_specs=[vmem] * len(pieces) + [pl.BlockSpec(memory_space=pltpu.SMEM)] * len(tables) + [vmem] * len(small),
        out_specs=(vmem,) * len(outs),
        scratch_shapes=[pltpu.VMEM((slots, order, order), jnp.bfloat16)] * 2,
        cost_estimate=pl.CostEstimate(
            flops=steps * 6 * 64 * order * order, transcendentals=0, bytes_accessed=steps * MATRIX_BYTES
        ),
        compiler_params=pltpu.CompilerParams(vmem_limit_bytes=(slots + 3) * MATRIX_BYTES),
    )(*here[: len(pieces)], *tables, *here[len(pieces) :])


def panel_of(x, y, core):
    return (x % SIDE * SIDE + y % SIDE) * 2 + core


def moved(block, phase, step):
    route = []
    for x in range(SIDE):
        for y in range(SIDE):
            for core in range(2):
                along_x = core == phase
                target = panel_of(x + step, y, core) if along_x else panel_of(x, y + step, core)
                route.append((panel_of(x, y, core), target))
    return lax.ppermute(block, "panel", route)


def line_of(rows):
    return [rows] + [moved(rows, 0, step) for step in STEPS]


def spread(line):
    return [line] + [moved(line, 1, step) for step in STEPS]


def flipped(pieces):
    flip = [(i, i ^ 1) for i in range(2 * SIDE * SIDE)]
    return pieces + [lax.ppermute(piece, "panel", flip) for piece in pieces]


def places_of(panel):
    x, y, core = panel // (2 * SIDE), panel // 2 % SIDE, panel % 2
    back = jnp.array((0,) + STEPS, jnp.int32)
    found = []
    for owner in (core, 1 - core):
        outer, inner = back[:, None], back[None, :]
        along_x = panel_of(x - inner + SIDE, y - outer + SIDE, 0)
        along_y = panel_of(x - outer + SIDE, y - inner + SIDE, 1)
        found.append(jnp.where(owner == 0, along_x, along_y).reshape(-1))
    return jnp.concatenate(found)


def gather_two_and_one(rows):
    line = line_of(rows)
    mine = spread(jnp.stack([block[:2] for block in line]))
    rest = jnp.stack([block[2:] for block in line])
    rest, *_ = lax.optimization_barrier((rest, *mine[1:]))
    return flipped(mine), spread(rest)


def after(pieces, value):
    *pieces, value = lax.optimization_barrier((*pieces, value))
    return flipped(pieces), value


def local(reflections, wave_decay, thickness, material):
    panel_rows = reflections.shape[1]
    order = reflections.shape[2]
    rows = (panel_rows, order)
    panel = lax.axis_index("panel")
    layer = lax.axis_index("layer")
    places = places_of(panel)
    inner = (layer == 1) | (layer == 2)
    inner_flag = inner.astype(jnp.int32)[None]
    facts = jnp.stack([panel * panel_rows, material[0]])
    own = lax.dynamic_index_in_dim(reflections, material[0], 0, keepdims=False)
    refl, trans = call(
        layer_kernel, 2 * TERMS, (rows, rows), flipped(spread(jnp.stack(line_of(own[None])))),
        (places, facts, thickness), (own, wave_decay),
    )
    pairs = [(0, 1), (1, 0), (2, 3), (3, 2)]
    oth_refl = lax.ppermute(refl, "layer", pairs)
    oth_trans = lax.ppermute(trans, "layer", pairs)
    pieces, closing = gather_two_and_one(jnp.stack([refl, oth_refl, trans]))
    (summed,) = call(pair_chain, 2 * TERMS, ((2 * panel_rows, order),), pieces, (places,), (trans, oth_trans))
    closing, summed = after(closing, summed)
    refl, trans, away = call(
        pair_close, 2, (rows, rows, rows), closing, (places, inner_flag), (summed, refl)
    )
    near = lax.ppermute(refl, "layer", [(1, 0), (2, 3)])
    cross = lax.ppermute(refl, "layer", [(1, 2), (2, 1)])
    far = lax.ppermute(away, "layer", [(0, 2), (2, 0), (1, 3), (3, 1)])
    near_trans = lax.ppermute(trans, "layer", [(1, 0), (2, 3)])
    pieces, closing = gather_two_and_one(
        jnp.stack(
            [jnp.where(inner, cross, near), jnp.where(inner, refl, far), jnp.where(inner, far, trans)]
        )
    )
    start = jnp.where(inner, trans, near_trans)
    (summed,) = call(last_chain, 2 * TERMS, (rows,), pieces, (places, inner_flag), (start,))
    closing, summed = after(closing, summed)
    (out,) = call(last_close, 2, (rows,), closing, (places, inner_flag), (summed, refl), placed=False)
    return out[None]


def solution(mesh):
    placed = (P(None, "panel", None), P(), P("layer"), P("layer"))
    return jax.shard_map(
        local, mesh=mesh, in_specs=placed, out_specs=P("layer", "panel", None), check_vma=False
    )
```

```python
import math

import jax
import jax.numpy as jnp
from jax import lax
from jax.experimental import pallas as pl
from jax.experimental.pallas import tpu as pltpu
from jax.sharding import PartitionSpec as P

TERMS = 6
SIDE = 4
STEPS = (1, 3, 2)
PIECES = 2 * SIDE
MATRIX_BYTES = 4 * 1024 * 1024


def halves(value):
    high = value.astype(jnp.bfloat16)
    low = (value - high.astype(jnp.float32)).astype(jnp.bfloat16)
    return high, low


def product(rows, high_ref, low_ref):
    count = rows.shape[0]
    high, low = halves(rows)
    both = jnp.concatenate([high, low], axis=0)
    by_high = jnp.dot(both, high_ref[...], preferred_element_type=jnp.float32)
    by_low = jnp.dot(high, low_ref[...], preferred_element_type=jnp.float32)
    return by_high[:count] + (by_high[count:] + by_low)


def split(pieces, places, high_ref, low_ref):
    lines, slots, panel_rows, _ = pieces[0].shape
    for i, piece in enumerate(pieces):

        def body(j, carry, i=i, piece=piece):
            rows = pl.ds(pl.multiple_of(places[i * lines + j] * panel_rows, panel_rows), panel_rows)
            for slot in range(slots):
                high, low = halves(piece[j, slot])
                high_ref[slot, rows, :] = high
                low_ref[slot, rows, :] = low
            return carry

        lax.fori_loop(0, lines, body, 0)


def layer_kernel(*refs):
    pieces, refs = refs[:PIECES], refs[PIECES:]
    wave_decay, places, facts, thickness, refl_out, trans_out, decays_out = refs[:7]
    high_out, low_out, high, low, decay_row, sem, sems = refs[7:]
    copy = pltpu.make_async_copy(wave_decay.at[pl.ds(facts[1], 1)], decay_row, sem)
    copy.start()
    split(pieces, places, high, low)
    saves = [pltpu.make_async_copy(high, high_out, sems.at[0]), pltpu.make_async_copy(low, low_out, sems.at[1])]
    for save in saves:
        save.start()
    copy.wait()
    rows, order = pieces[0].shape[2:]
    decays = jnp.exp(-decay_row[...] * thickness[0])
    decays_out[...] = decays
    row_ids = facts[0] + lax.broadcasted_iota(jnp.int32, (rows, order), 0)
    eye = row_ids == lax.broadcasted_iota(jnp.int32, (rows, order), 1)
    own_decays = jnp.sum(jnp.where(eye, decays, 0.0), axis=1, keepdims=True)
    term = product(own_decays * pieces[0][0, 0] * decays, high.at[0], low.at[0])

    def body(k, carry):
        term, summed = carry
        term = product(term * decays, high.at[0], low.at[0])
        term = product(term * decays, high.at[0], low.at[0])
        return term, summed + term

    _, summed = lax.fori_loop(0, TERMS - 2, body, (term, jnp.where(eye, 1.0, 0.0) + term))
    scaled = summed * decays
    both = product(jnp.concatenate([scaled, summed], axis=0), high.at[0], low.at[0])
    refl_out[...] = both[:rows] * decays - both[rows:]
    trans_out[...] = scaled - product(both[:rows], high.at[0], low.at[0])
    for save in saves:
        save.wait()


def pair_kernel(*refs):
    own_pieces, oth_pieces, refs = refs[:PIECES], refs[PIECES : 2 * PIECES], refs[2 * PIECES :]
    high_in, low_in, places, inner, own_refl, own_trans, oth_trans, decay_row = refs[:8]
    refl_out, trans_out, far_out, own_high, own_low, oth_high, oth_low, layer_high, layer_low, sems = refs[8:]
    loads = [
        pltpu.make_async_copy(high_in, layer_high, sems.at[0]),
        pltpu.make_async_copy(low_in, layer_low, sems.at[1]),
    ]
    for load in loads:
        load.start()
    split(own_pieces, places, own_high, own_low)
    split(oth_pieces, places, oth_high, oth_low)
    first = product(own_trans[...], oth_high.at[0], oth_low.at[0])
    both = jnp.concatenate([first, oth_trans[...]], axis=0)

    def chain(k, carry):
        both, summed = carry
        both = product(both, own_high.at[0], own_low.at[0])
        both = product(both, oth_high.at[0], oth_low.at[0])
        return both, summed + both

    _, summed = lax.fori_loop(0, TERMS - 1, chain, (both, both))
    decays = decay_row[...]
    for load in loads:
        load.wait()

    def layer(rows):
        return product(rows, layer_high.at[0], layer_low.at[0])

    def series(k, carry):
        term, summed = carry
        term = layer(layer(term * decays) * decays)
        return term, summed + term

    _, summed = lax.fori_loop(0, TERMS - 1, series, (summed, summed))
    scaled = summed * decays
    done = scaled - layer(layer(scaled))
    rows = own_refl.shape[0]
    refl, trans = own_refl[...] + done[:rows], done[rows:]
    refl_out[...] = refl
    trans_out[...] = trans
    far_out[...] = jnp.where(inner[0] == 1, refl, trans)


def last_chain(*refs):
    pieces, refs = refs[:PIECES], refs[PIECES:]
    places, inner, start, out, high, low = refs
    split(pieces, places, high, low)
    first, second = 1 - inner[0], inner[0]
    term = start[...]
    half = product(term, high.at[first], low.at[first])

    def body(k, carry):
        half, term_sum, half_sum = carry
        term = product(half, high.at[second], low.at[second])
        half = product(term, high.at[first], low.at[first])
        return half, term_sum + term, half_sum + half

    _, term_sum, half_sum = lax.fori_loop(0, TERMS - 1, body, (half, term, half))
    out[...] = jnp.where(inner[0] == 1, term_sum, half_sum)


def last_close(*refs):
    pieces, refs = refs[:PIECES], refs[PIECES:]
    places, inner, summed, own_refl, out, high, low = refs
    split(pieces, places, high, low)
    base = jnp.where(inner[0] == 1, 0.0, own_refl[...])
    out[...] = base + product(summed[...], high.at[0], low.at[0])


def call(kernel, room, steps, outs, pieces, tables, small, far=(), scratch=(), placed=True):
    vmem = pl.BlockSpec(memory_space=pltpu.VMEM)
    here = [pltpu.with_memory_space_constraint(a, pltpu.VMEM) for a in (*pieces, *small)]
    far = [pltpu.with_memory_space_constraint(a, pltpu.HBM) for a in far]
    used = sum(math.prod(a.shape) * 2 for a in scratch if len(a.shape) == 3)
    return pl.pallas_call(
        kernel,
        out_shape=tuple(
            out if placed else jax.ShapeDtypeStruct(out.shape, out.dtype) for out in outs
        ),
        in_specs=[vmem] * len(pieces)
        + [pl.BlockSpec(memory_space=pl.ANY)] * len(far)
        + [pl.BlockSpec(memory_space=pltpu.SMEM)] * len(tables)
        + [vmem] * len(small),
        out_specs=tuple(vmem if out.dtype == jnp.float32 else pl.BlockSpec(memory_space=pl.ANY) for out in outs),
        scratch_shapes=list(scratch),
        cost_estimate=pl.CostEstimate(
            flops=steps * 6 * 64 * 1024 * 1024, transcendentals=0, bytes_accessed=steps * MATRIX_BYTES
        ),
        compiler_params=pltpu.CompilerParams(vmem_limit_bytes=used + room * 1024 * 1024),
    )(*here[: len(pieces)], *far, *tables, *here[len(pieces) :])


def matrices(slots, order, space=pltpu.VMEM):
    return (space((slots, order, order), jnp.bfloat16),) * 2


def panel_of(x, y, core):
    return (x % SIDE * SIDE + y % SIDE) * 2 + core


def moved(block, phase, step):
    route = []
    for x in range(SIDE):
        for y in range(SIDE):
            for core in range(2):
                along_x = core == phase
                target = panel_of(x + step, y, core) if along_x else panel_of(x, y + step, core)
                route.append((panel_of(x, y, core), target))
    return lax.ppermute(block, "panel", route)


def line_of(rows):
    return [rows] + [moved(rows, 0, step) for step in STEPS]


def spread(line):
    return [line] + [moved(line, 1, step) for step in STEPS]


def flipped(pieces):
    flip = [(i, i ^ 1) for i in range(2 * SIDE * SIDE)]
    return pieces + [lax.ppermute(piece, "panel", flip) for piece in pieces]


def places_of(panel):
    x, y, core = panel // (2 * SIDE), panel // 2 % SIDE, panel % 2
    back = jnp.array((0,) + STEPS, jnp.int32)
    found = []
    for owner in (core, 1 - core):
        outer, inner = back[:, None], back[None, :]
        along_x = panel_of(x - inner + SIDE, y - outer + SIDE, 0)
        along_y = panel_of(x - outer + SIDE, y - inner + SIDE, 1)
        found.append(jnp.where(owner == 0, along_x, along_y).reshape(-1))
    return jnp.concatenate(found)


def after(pieces, value):
    *pieces, value = lax.optimization_barrier((*pieces, value))
    return flipped(pieces), value


def local(reflections, wave_decay, thickness, material):
    panel_rows = reflections.shape[1]
    order = reflections.shape[2]
    rows = (panel_rows, order)
    panel = lax.axis_index("panel")
    layer = lax.axis_index("layer")
    places = places_of(panel)
    inner = (layer == 1) | (layer == 2)
    inner_flag = inner.astype(jnp.int32)[None]
    facts = jnp.stack([panel * panel_rows, material[0]])
    own = lax.dynamic_index_in_dim(reflections, material[0], 0, keepdims=False)
    block = pltpu.VMEM(rows, jnp.float32)
    refl, trans, decays, *halved = call(
        layer_kernel, 10, 2 * TERMS, (block, block, pltpu.VMEM((1, order), jnp.float32), *matrices(1, order, pltpu.HBM)),
        flipped(spread(jnp.stack(line_of(own[None])))), (places, facts, thickness), (), far=(wave_decay,),
        scratch=(
            *matrices(1, order), pltpu.VMEM((1, order), jnp.float32),
            pltpu.SemaphoreType.DMA(()), pltpu.SemaphoreType.DMA((2,)),
        ),
    )
    pairs = [(0, 1), (1, 0), (2, 3), (3, 2)]
    line = jnp.stack(line_of(refl[None]))
    oth_line = lax.ppermute(line, "layer", pairs)
    oth_trans = lax.ppermute(trans, "layer", pairs)
    mine = spread(line)
    oth_line, oth_trans, mine[3] = lax.optimization_barrier((oth_line, oth_trans, mine[3]))
    refl, trans, away = call(
        pair_kernel, 16, 4 * TERMS, (block, block, block), flipped(mine) + flipped(spread(oth_line)),
        (places, inner_flag), (refl, trans, oth_trans, decays), far=halved,
        scratch=matrices(1, order) * 3 + (pltpu.SemaphoreType.DMA((2,)),),
    )
    far = lax.ppermute(away, "layer", [(0, 2), (2, 0), (1, 3), (3, 1)])
    near = lax.ppermute(refl, "layer", [(1, 0), (2, 3)])
    cross = lax.ppermute(refl, "layer", [(1, 2), (2, 1)])
    blocks = jnp.stack(
        [jnp.where(inner, cross, near), jnp.where(inner, refl, far), jnp.where(inner, far, trans)]
    )
    trans, blocks = lax.optimization_barrier((trans, blocks))
    near_trans = lax.ppermute(trans, "layer", [(1, 0), (2, 3)])
    line = line_of(blocks)
    mine = spread(jnp.stack([part[:2] for part in line]))
    rest = jnp.stack([part[2:] for part in line])
    rest, *_ = lax.optimization_barrier((rest, *mine[1:]))
    rest = spread(rest)
    start = jnp.where(inner, trans, near_trans)
    (summed,) = call(
        last_chain, 12, 2 * TERMS, (block,), flipped(mine), (places, inner_flag), (start,), scratch=matrices(2, order)
    )
    closing, summed = after(rest, summed)
    (out,) = call(
        last_close, 10, 2, (block,), closing, (places, inner_flag), (summed, refl), scratch=matrices(1, order), placed=False
    )
    return out[None]


def solution(mesh):
    placed = (P(None, "panel", None), P(), P("layer"), P("layer"))
    return jax.shard_map(
        local, mesh=mesh, in_specs=placed, out_specs=P("layer", "panel", None), check_vma=False
    )
```

```python
import math

import jax
import jax.numpy as jnp
from jax import lax
from jax.experimental import pallas as pl
from jax.experimental.pallas import tpu as pltpu
from jax.sharding import PartitionSpec as P

TERMS = 6
SIDE = 4
STEPS = (1, 3, 2)
PIECES = 2 * SIDE
FEW_ROWS = 32
MATRIX_BYTES = 4 * 1024 * 1024


def halves(value):
    high = value.astype(jnp.bfloat16)
    low = (value - high.astype(jnp.float32)).astype(jnp.bfloat16)
    return high, low


def product(rows, high_ref, low_ref):
    count = rows.shape[0]
    high, low = halves(rows)
    both = jnp.concatenate([high, low], axis=0)
    by_high = jnp.dot(both, high_ref[...], preferred_element_type=jnp.float32)
    by_low = jnp.dot(both if count > FEW_ROWS else high, low_ref[...], preferred_element_type=jnp.float32)
    if count > FEW_ROWS:
        done = by_high + by_low
        return done[:count] + done[count:]
    return by_high[:count] + (by_high[count:] + by_low)


def split(pieces, places, high_ref, low_ref):
    before = 0
    for piece in pieces:
        lines, slots, panel_rows, _ = piece.shape

        def body(j, carry, before=before, piece=piece):
            rows = pl.ds(pl.multiple_of(places[before + j] * panel_rows, panel_rows), panel_rows)
            for slot in range(slots):
                high, low = halves(piece[j, slot])
                high_ref[slot, rows, :] = high
                low_ref[slot, rows, :] = low
            return carry

        lax.fori_loop(0, lines, body, 0)
        before += lines


def layer_kernel(*refs):
    pieces, refs = refs[:PIECES], refs[PIECES:]
    wave_decay, places, facts, thickness, refl_out, trans_out, decays_out = refs[:7]
    high_out, low_out, high, low, decay_row, sem, sems = refs[7:]
    copy = pltpu.make_async_copy(wave_decay.at[pl.ds(facts[1], 1)], decay_row, sem)
    copy.start()
    split(pieces, places, high, low)
    saves = [pltpu.make_async_copy(high, high_out, sems.at[0]), pltpu.make_async_copy(low, low_out, sems.at[1])]
    for save in saves:
        save.start()
    copy.wait()
    rows, order = pieces[0].shape[2:]
    decays = jnp.exp(-decay_row[...] * thickness[0])
    decays_out[...] = decays
    row_ids = facts[0] + lax.broadcasted_iota(jnp.int32, (rows, order), 0)
    eye = row_ids == lax.broadcasted_iota(jnp.int32, (rows, order), 1)
    own_decays = jnp.sum(jnp.where(eye, decays, 0.0), axis=1, keepdims=True)
    term = product(own_decays * pieces[0][0, 0] * decays, high.at[0], low.at[0])

    def body(k, carry):
        term, summed = carry
        term = product(term * decays, high.at[0], low.at[0])
        term = product(term * decays, high.at[0], low.at[0])
        return term, summed + term

    _, summed = lax.fori_loop(0, TERMS - 2, body, (term, jnp.where(eye, 1.0, 0.0) + term))
    scaled = summed * decays
    both = product(jnp.concatenate([scaled, summed], axis=0), high.at[0], low.at[0])
    refl_out[...] = both[:rows] * decays - both[rows:]
    trans_out[...] = scaled - product(both[:rows], high.at[0], low.at[0])
    for save in saves:
        save.wait()


def pair_kernel(*refs):
    own_pieces, oth_pieces, refs = refs[:PIECES], refs[PIECES : 2 * PIECES], refs[2 * PIECES :]
    high_in, low_in, places, inner, own_refl, own_trans, oth_trans, decay_row = refs[:8]
    refl_out, trans_out, far_out, own_high, own_low, oth_high, oth_low, layer_high, layer_low, sems = refs[8:]
    loads = [
        pltpu.make_async_copy(high_in, layer_high, sems.at[0]),
        pltpu.make_async_copy(low_in, layer_low, sems.at[1]),
    ]
    for load in loads:
        load.start()
    split(own_pieces, places, own_high, own_low)
    split(oth_pieces, places, oth_high, oth_low)
    first = product(own_trans[...], oth_high.at[0], oth_low.at[0])
    both = jnp.concatenate([first, oth_trans[...]], axis=0)

    def chain(k, carry):
        both, summed = carry
        both = product(both, own_high.at[0], own_low.at[0])
        both = product(both, oth_high.at[0], oth_low.at[0])
        return both, summed + both

    _, summed = lax.fori_loop(0, TERMS - 1, chain, (both, both))
    decays = decay_row[...]
    for load in loads:
        load.wait()

    def layer(rows):
        return product(rows, layer_high.at[0], layer_low.at[0])

    def series(k, carry):
        term, summed = carry
        term = layer(layer(term * decays) * decays)
        return term, summed + term

    _, summed = lax.fori_loop(0, TERMS - 1, series, (summed, summed))
    scaled = summed * decays
    done = scaled - layer(layer(scaled))
    rows = own_refl.shape[0]
    refl, trans = own_refl[...] + done[:rows], done[rows:]
    refl_out[...] = refl
    trans_out[...] = trans
    far_out[...] = jnp.where(inner[0] == 1, refl, trans)


def last_chain(*refs):
    pieces, refs = refs[:PIECES], refs[PIECES:]
    places, inner, own_trans, near_trans, out, high, low = refs
    split(pieces, places, high, low)
    first, second = 1 - inner[0], inner[0]
    term = jnp.where(inner[0] == 1, own_trans[...], near_trans[...])
    half = product(term, high.at[first], low.at[first])

    def body(k, carry):
        half, term_sum, half_sum = carry
        term = product(half, high.at[second], low.at[second])
        half = product(term, high.at[first], low.at[first])
        return half, term_sum + term, half_sum + half

    _, term_sum, half_sum = lax.fori_loop(0, TERMS - 1, body, (half, term, half))
    out[...] = jnp.where(inner[0] == 1, term_sum, half_sum)


def last_close(*refs):
    pieces, refs = refs[:SIDE], refs[SIDE:]
    places, summed, oth_summed, own_out, oth_out, high, low = refs
    split(pieces, places, high, low)
    rows, order = summed.shape
    empty = jnp.zeros((rows, order), jnp.bfloat16)

    def clear(j, carry):
        part = pl.ds(pl.multiple_of(places[SIDE * SIDE + j] * rows, rows), rows)
        high[0, part, :] = empty
        low[0, part, :] = empty
        return carry

    lax.fori_loop(0, SIDE * SIDE, clear, 0)
    both = jnp.concatenate([summed[...], oth_summed[...]], axis=0)
    done = product(both, high.at[0], low.at[0])
    own_out[...] = done[:rows]
    oth_out[...] = done[rows:]


def call(kernel, room, steps, outs, pieces, tables, small, far=(), scratch=(), placed=True):
    vmem = pl.BlockSpec(memory_space=pltpu.VMEM)
    here = [pltpu.with_memory_space_constraint(a, pltpu.VMEM) for a in (*pieces, *small)]
    far = [pltpu.with_memory_space_constraint(a, pltpu.HBM) for a in far]
    used = sum(math.prod(a.shape) * 2 for a in scratch if len(a.shape) == 3)
    return pl.pallas_call(
        kernel,
        out_shape=tuple(
            out if placed else jax.ShapeDtypeStruct(out.shape, out.dtype) for out in outs
        ),
        in_specs=[vmem] * len(pieces)
        + [pl.BlockSpec(memory_space=pl.ANY)] * len(far)
        + [pl.BlockSpec(memory_space=pltpu.SMEM)] * len(tables)
        + [vmem] * len(small),
        out_specs=tuple(vmem if out.dtype == jnp.float32 else pl.BlockSpec(memory_space=pl.ANY) for out in outs),
        scratch_shapes=list(scratch),
        cost_estimate=pl.CostEstimate(
            flops=steps * 6 * 64 * 1024 * 1024, transcendentals=0, bytes_accessed=steps * MATRIX_BYTES
        ),
        compiler_params=pltpu.CompilerParams(vmem_limit_bytes=used + room * 1024 * 1024),
    )(*here[: len(pieces)], *far, *tables, *here[len(pieces) :])


def matrices(slots, order, space=pltpu.VMEM):
    return (space((slots, order, order), jnp.bfloat16),) * 2


def panel_of(x, y, core):
    return (x % SIDE * SIDE + y % SIDE) * 2 + core


def moved(block, phase, step):
    route = []
    for x in range(SIDE):
        for y in range(SIDE):
            for core in range(2):
                along_x = core == phase
                target = panel_of(x + step, y, core) if along_x else panel_of(x, y + step, core)
                route.append((panel_of(x, y, core), target))
    return lax.ppermute(block, "panel", route)


def line_of(rows):
    return [rows] + [moved(rows, 0, step) for step in STEPS]


def spread(line):
    return [line] + [moved(line, 1, step) for step in STEPS]


def other_core(block):
    return lax.ppermute(block, "panel", [(i, i ^ 1) for i in range(2 * SIDE * SIDE)])


def flipped(pieces):
    return pieces + [other_core(piece) for piece in pieces]


def places_of(panel):
    x, y, core = panel // (2 * SIDE), panel // 2 % SIDE, panel % 2
    back = jnp.array((0,) + STEPS, jnp.int32)
    found = []
    for owner in (core, 1 - core):
        outer, inner = back[:, None], back[None, :]
        along_x = panel_of(x - inner + SIDE, y - outer + SIDE, 0)
        along_y = panel_of(x - outer + SIDE, y - inner + SIDE, 1)
        found.append(jnp.where(owner == 0, along_x, along_y).reshape(-1))
    return jnp.concatenate(found)


def local(reflections, wave_decay, thickness, material):
    panel_rows = reflections.shape[1]
    order = reflections.shape[2]
    rows = (panel_rows, order)
    panel = lax.axis_index("panel")
    layer = lax.axis_index("layer")
    places = places_of(panel)
    inner = (layer == 1) | (layer == 2)
    inner_flag = inner.astype(jnp.int32)[None]
    facts = jnp.stack([panel * panel_rows, material[0]])
    own = lax.dynamic_index_in_dim(reflections, material[0], 0, keepdims=False)
    block = pltpu.VMEM(rows, jnp.float32)
    refl, trans, decays, *halved = call(
        layer_kernel, 10, 2 * TERMS, (block, block, pltpu.VMEM((1, order), jnp.float32), *matrices(1, order, pltpu.HBM)),
        flipped(spread(jnp.stack(line_of(own[None])))), (places, facts, thickness), (), far=(wave_decay,),
        scratch=(
            *matrices(1, order), pltpu.VMEM((1, order), jnp.float32),
            pltpu.SemaphoreType.DMA(()), pltpu.SemaphoreType.DMA((2,)),
        ),
    )
    pairs = [(0, 1), (1, 0), (2, 3), (3, 2)]
    line = jnp.stack(line_of(refl[None]))
    oth_line = lax.ppermute(line, "layer", pairs)
    oth_trans = lax.ppermute(trans, "layer", pairs)
    mine = spread(line)
    oth_line, oth_trans, mine[3] = lax.optimization_barrier((oth_line, oth_trans, mine[3]))
    refl, trans, away = call(
        pair_kernel, 16, 4 * TERMS, (block, block, block), flipped(mine) + flipped(spread(oth_line)),
        (places, inner_flag), (refl, trans, oth_trans, decays), far=halved,
        scratch=matrices(1, order) * 3 + (pltpu.SemaphoreType.DMA((2,)),),
    )
    far = lax.ppermute(away, "layer", [(0, 2), (2, 0), (1, 3), (3, 1)])
    near = lax.ppermute(refl, "layer", [(1, 0), (2, 3)])
    cross = lax.ppermute(refl, "layer", [(1, 2), (2, 1)])
    blocks = jnp.stack(
        [jnp.where(inner, cross, near), jnp.where(inner, refl, far), jnp.where(inner, far, trans)]
    )
    trans, blocks = lax.optimization_barrier((trans, blocks))
    near_trans = lax.ppermute(trans, "layer", [(1, 0), (2, 3)])
    line = line_of(blocks)
    mine = spread(jnp.stack([part[:2] for part in line]))
    rest = jnp.stack([part[2:] for part in line])
    rest, *_ = lax.optimization_barrier((rest, *mine[1:]))
    rest = spread(rest)
    (summed,) = call(
        last_chain, 12, 2 * TERMS, (block,), flipped(mine), (places, inner_flag), (trans, near_trans), scratch=matrices(2, order)
    )
    *rest, summed = lax.optimization_barrier((*rest, summed))
    own_part, oth_part = call(
        last_close, 10, 2, (block, block), rest, (places,), (summed, other_core(summed)), scratch=matrices(1, order)
    )
    out = jnp.where(inner, 0.0, refl) + (own_part + other_core(oth_part))
    return out[None]


def solution(mesh):
    placed = (P(None, "panel", None), P(), P("layer"), P("layer"))
    return jax.shard_map(
        local, mesh=mesh, in_specs=placed, out_specs=P("layer", "panel", None), check_vma=False
    )
```

```python
import math

import jax
import jax.numpy as jnp
from jax import lax
from jax.experimental import pallas as pl
from jax.experimental.pallas import tpu as pltpu
from jax.sharding import PartitionSpec as P

TERMS = 6
SIDE = 4
STEPS = (1, 3, 2)
PIECES = 2 * SIDE
FEW_ROWS = 32
MATRIX_BYTES = 4 * 1024 * 1024


def halves(value):
    high = value.astype(jnp.bfloat16)
    low = (value - high.astype(jnp.float32)).astype(jnp.bfloat16)
    return high, low


def product(rows, high_ref, low_ref):
    count = rows.shape[0]
    high, low = halves(rows)
    both = jnp.concatenate([high, low], axis=0)
    by_high = jnp.dot(both, high_ref[...], preferred_element_type=jnp.float32)
    by_low = jnp.dot(both if count > FEW_ROWS else high, low_ref[...], preferred_element_type=jnp.float32)
    if count > FEW_ROWS:
        done = by_high + by_low
        return done[:count] + done[count:]
    return by_high[:count] + (by_high[count:] + by_low)


def split(pieces, places, high_ref, low_ref, before=0):
    for piece in pieces:
        lines, slots, panel_rows, _ = piece.shape

        def body(j, carry, before=before, piece=piece):
            rows = pl.ds(pl.multiple_of(places[before + j] * panel_rows, panel_rows), panel_rows)
            for slot in range(slots):
                high, low = halves(piece[j, slot])
                high_ref[slot, rows, :] = high
                low_ref[slot, rows, :] = low
            return carry

        lax.fori_loop(0, lines, body, 0)
        before += lines


def layer_kernel(*refs):
    pieces, refs = refs[:PIECES], refs[PIECES:]
    wave_decay, places, facts, thickness, refl_out, trans_out, decays_out = refs[:7]
    high_out, low_out, high, low, decay_row, sem, sems = refs[7:]
    copy = pltpu.make_async_copy(wave_decay.at[pl.ds(facts[1], 1)], decay_row, sem)
    copy.start()
    split(pieces, places, high, low)
    saves = [pltpu.make_async_copy(high, high_out, sems.at[0]), pltpu.make_async_copy(low, low_out, sems.at[1])]
    for save in saves:
        save.start()
    copy.wait()
    rows, order = pieces[0].shape[2:]
    decays = jnp.exp(-decay_row[...] * thickness[0])
    decays_out[...] = decays
    row_ids = facts[0] + lax.broadcasted_iota(jnp.int32, (rows, order), 0)
    eye = row_ids == lax.broadcasted_iota(jnp.int32, (rows, order), 1)
    own_decays = jnp.sum(jnp.where(eye, decays, 0.0), axis=1, keepdims=True)
    term = product(own_decays * pieces[0][0, 0] * decays, high.at[0], low.at[0])

    def body(k, carry):
        term, summed = carry
        term = product(term * decays, high.at[0], low.at[0])
        term = product(term * decays, high.at[0], low.at[0])
        return term, summed + term

    _, summed = lax.fori_loop(0, TERMS - 2, body, (term, jnp.where(eye, 1.0, 0.0) + term))
    scaled = summed * decays
    both = product(jnp.concatenate([scaled, summed], axis=0), high.at[0], low.at[0])
    refl_out[...] = both[:rows] * decays - both[rows:]
    trans_out[...] = scaled - product(both[:rows], high.at[0], low.at[0])
    for save in saves:
        save.wait()


def pair_kernel(*refs):
    own_pieces, oth_pieces, refs = refs[: PIECES - 1], refs[PIECES - 1 : 2 * PIECES - 2], refs[2 * PIECES - 2 :]
    high_in, low_in, own_far, oth_far, places, inner, own_refl, own_trans, oth_trans, decay_row = refs[:10]
    refl_out, trans_out, far_out, own_high, own_low, oth_high, oth_low, layer_high, layer_low, stage, sems = refs[10:]
    brought = [
        pltpu.make_async_copy(own_far, stage.at[0], sems.at[2]),
        pltpu.make_async_copy(oth_far, stage.at[1], sems.at[3]),
    ]
    for load in brought:
        load.start()
    loads = [
        pltpu.make_async_copy(high_in, layer_high, sems.at[0]),
        pltpu.make_async_copy(low_in, layer_low, sems.at[1]),
    ]
    for load in loads:
        load.start()
    split(own_pieces, places, own_high, own_low)
    split(oth_pieces[:SIDE], places, oth_high, oth_low)
    split(oth_pieces[SIDE:], places, oth_high, oth_low, before=(SIDE + 1) * SIDE)
    for load in brought:
        load.wait()
    split([stage.at[0]], places, own_high, own_low, before=(PIECES - 1) * SIDE)
    split([stage.at[1]], places, oth_high, oth_low, before=SIDE * SIDE)
    first = product(own_trans[...], oth_high.at[0], oth_low.at[0])
    both = jnp.concatenate([first, oth_trans[...]], axis=0)

    def chain(k, carry):
        both, summed = carry
        both = product(both, own_high.at[0], own_low.at[0])
        both = product(both, oth_high.at[0], oth_low.at[0])
        return both, summed + both

    _, summed = lax.fori_loop(0, TERMS - 1, chain, (both, both))
    decays = decay_row[...]
    for load in loads:
        load.wait()

    def layer(rows):
        return product(rows, layer_high.at[0], layer_low.at[0])

    def series(k, carry):
        term, summed = carry
        term = layer(layer(term * decays) * decays)
        return term, summed + term

    _, summed = lax.fori_loop(0, TERMS - 1, series, (summed, summed))
    scaled = summed * decays
    done = scaled - layer(layer(scaled))
    rows = own_refl.shape[0]
    refl, trans = own_refl[...] + done[:rows], done[rows:]
    refl_out[...] = refl
    trans_out[...] = trans
    far_out[...] = jnp.where(inner[0] == 1, refl, trans)


def last_chain(*refs):
    pieces, refs = refs[:PIECES], refs[PIECES:]
    places, inner, own_trans, near_trans, out, high, low = refs
    split(pieces, places, high, low)
    first, second = 1 - inner[0], inner[0]
    term = jnp.where(inner[0] == 1, own_trans[...], near_trans[...])
    half = product(term, high.at[first], low.at[first])

    def body(k, carry):
        half, term_sum, half_sum = carry
        term = product(half, high.at[second], low.at[second])
        half = product(term, high.at[first], low.at[first])
        return half, term_sum + term, half_sum + half

    _, term_sum, half_sum = lax.fori_loop(0, TERMS - 1, body, (half, term, half))
    out[...] = jnp.where(inner[0] == 1, term_sum, half_sum)


def last_close(*refs):
    pieces, refs = refs[:SIDE], refs[SIDE:]
    places, summed, oth_summed, own_out, oth_out, high, low = refs
    split(pieces, places, high, low)
    rows, order = summed.shape
    empty = jnp.zeros((rows, order), jnp.bfloat16)

    def clear(j, carry):
        part = pl.ds(pl.multiple_of(places[SIDE * SIDE + j] * rows, rows), rows)
        high[0, part, :] = empty
        low[0, part, :] = empty
        return carry

    lax.fori_loop(0, SIDE * SIDE, clear, 0)
    both = jnp.concatenate([summed[...], oth_summed[...]], axis=0)
    done = product(both, high.at[0], low.at[0])
    own_out[...] = done[:rows]
    oth_out[...] = done[rows:]


def call(kernel, room, steps, outs, pieces, tables, small, far=(), scratch=(), placed=True):
    vmem = pl.BlockSpec(memory_space=pltpu.VMEM)
    here = [pltpu.with_memory_space_constraint(a, pltpu.VMEM) for a in (*pieces, *small)]
    far = [pltpu.with_memory_space_constraint(a, pltpu.HBM) for a in far]
    used = sum(math.prod(a.shape) * 2 for a in scratch if len(a.shape) == 3)
    return pl.pallas_call(
        kernel,
        out_shape=tuple(
            out if placed else jax.ShapeDtypeStruct(out.shape, out.dtype) for out in outs
        ),
        in_specs=[vmem] * len(pieces)
        + [pl.BlockSpec(memory_space=pl.ANY)] * len(far)
        + [pl.BlockSpec(memory_space=pltpu.SMEM)] * len(tables)
        + [vmem] * len(small),
        out_specs=tuple(vmem if out.dtype == jnp.float32 else pl.BlockSpec(memory_space=pl.ANY) for out in outs),
        scratch_shapes=list(scratch),
        cost_estimate=pl.CostEstimate(
            flops=steps * 6 * 64 * 1024 * 1024, transcendentals=0, bytes_accessed=steps * MATRIX_BYTES
        ),
        compiler_params=pltpu.CompilerParams(vmem_limit_bytes=used + room * 1024 * 1024),
    )(*here[: len(pieces)], *far, *tables, *here[len(pieces) :])


def matrices(slots, order, space=pltpu.VMEM):
    return (space((slots, order, order), jnp.bfloat16),) * 2


def panel_of(x, y, core):
    return (x % SIDE * SIDE + y % SIDE) * 2 + core


def moved(block, phase, step):
    route = []
    for x in range(SIDE):
        for y in range(SIDE):
            for core in range(2):
                along_x = core == phase
                target = panel_of(x + step, y, core) if along_x else panel_of(x, y + step, core)
                route.append((panel_of(x, y, core), target))
    return lax.ppermute(block, "panel", route)


def line_of(rows):
    return [rows] + [moved(rows, 0, step) for step in STEPS]


def spread(line):
    return [line] + [moved(line, 1, step) for step in STEPS]


def other_core(block):
    return lax.ppermute(block, "panel", [(i, i ^ 1) for i in range(2 * SIDE * SIDE)])


def flipped(pieces):
    return pieces + [other_core(piece) for piece in pieces]


def places_of(panel):
    x, y, core = panel // (2 * SIDE), panel // 2 % SIDE, panel % 2
    back = jnp.array((0,) + STEPS, jnp.int32)
    found = []
    for owner in (core, 1 - core):
        outer, inner = back[:, None], back[None, :]
        along_x = panel_of(x - inner + SIDE, y - outer + SIDE, 0)
        along_y = panel_of(x - outer + SIDE, y - inner + SIDE, 1)
        found.append(jnp.where(owner == 0, along_x, along_y).reshape(-1))
    return jnp.concatenate(found)


def local(reflections, wave_decay, thickness, material):
    panel_rows = reflections.shape[1]
    order = reflections.shape[2]
    rows = (panel_rows, order)
    panel = lax.axis_index("panel")
    layer = lax.axis_index("layer")
    places = places_of(panel)
    inner = (layer == 1) | (layer == 2)
    inner_flag = inner.astype(jnp.int32)[None]
    facts = jnp.stack([panel * panel_rows, material[0]])
    own = lax.dynamic_index_in_dim(reflections, material[0], 0, keepdims=False)
    block = pltpu.VMEM(rows, jnp.float32)
    refl, trans, decays, *halved = call(
        layer_kernel, 10, 2 * TERMS, (block, block, pltpu.VMEM((1, order), jnp.float32), *matrices(1, order, pltpu.HBM)),
        flipped(spread(jnp.stack(line_of(own[None])))), (places, facts, thickness), (), far=(wave_decay,),
        scratch=(
            *matrices(1, order), pltpu.VMEM((1, order), jnp.float32),
            pltpu.SemaphoreType.DMA(()), pltpu.SemaphoreType.DMA((2,)),
        ),
    )
    pairs = [(0, 1), (1, 0), (2, 3), (3, 2)]
    line = jnp.stack(line_of(refl[None]))
    oth_line = lax.ppermute(line, "layer", pairs)
    oth_trans = lax.ppermute(trans, "layer", pairs)
    mine = spread(line)
    oth_line, oth_trans, mine[3] = lax.optimization_barrier((oth_line, oth_trans, mine[3]))
    own_pieces, oth_pieces = flipped(mine), flipped(spread(oth_line))
    refl, trans, away = call(
        pair_kernel, 16, 4 * TERMS, (block, block, block),
        own_pieces[: PIECES - 1] + oth_pieces[:SIDE] + oth_pieces[SIDE + 1 :], (places, inner_flag),
        (refl, trans, oth_trans, decays), far=(*halved, own_pieces[PIECES - 1], oth_pieces[SIDE]),
        scratch=matrices(1, order) * 3
        + (pltpu.VMEM((2, SIDE, 1, *rows), jnp.float32), pltpu.SemaphoreType.DMA((4,))),
    )
    far = lax.ppermute(away, "layer", [(0, 2), (2, 0), (1, 3), (3, 1)])
    near = lax.ppermute(refl, "layer", [(1, 0), (2, 3)])
    cross = lax.ppermute(refl, "layer", [(1, 2), (2, 1)])
    blocks = jnp.stack(
        [jnp.where(inner, cross, near), jnp.where(inner, refl, far), jnp.where(inner, far, trans)]
    )
    trans, blocks = lax.optimization_barrier((trans, blocks))
    near_trans = lax.ppermute(trans, "layer", [(1, 0), (2, 3)])
    line = line_of(blocks)
    mine = spread(jnp.stack([part[:2] for part in line]))
    rest = jnp.stack([part[2:] for part in line])
    rest, *_ = lax.optimization_barrier((rest, *mine[1:]))
    rest = spread(rest)
    (summed,) = call(
        last_chain, 12, 2 * TERMS, (block,), flipped(mine), (places, inner_flag), (trans, near_trans), scratch=matrices(2, order)
    )
    *rest, summed = lax.optimization_barrier((*rest, summed))
    own_part, oth_part = call(
        last_close, 10, 2, (block, block), rest, (places,), (summed, other_core(summed)), scratch=matrices(1, order)
    )
    out = jnp.where(inner, 0.0, refl) + (own_part + other_core(oth_part))
    return out[None]


def solution(mesh):
    placed = (P(None, "panel", None), P(), P("layer"), P("layer"))
    return jax.shard_map(
        local, mesh=mesh, in_specs=placed, out_specs=P("layer", "panel", None), check_vma=False
    )
```

```python
import math

import jax
import jax.numpy as jnp
from jax import lax
from jax.experimental import pallas as pl
from jax.experimental.pallas import tpu as pltpu
from jax.sharding import PartitionSpec as P

TERMS = 6
SIDE = 4
STEPS = (1, 3, 2)
PIECES = 2 * SIDE
FEW_ROWS = 32
MATRIX_BYTES = 4 * 1024 * 1024


def halves(value):
    high = value.astype(jnp.bfloat16)
    low = (value - high.astype(jnp.float32)).astype(jnp.bfloat16)
    return high, low


def product(rows, high_ref, low_ref):
    count = rows.shape[0]
    high, low = halves(rows)
    both = jnp.concatenate([high, low], axis=0)
    by_high = jnp.dot(both, high_ref[...], preferred_element_type=jnp.float32)
    by_low = jnp.dot(both if count > FEW_ROWS else high, low_ref[...], preferred_element_type=jnp.float32)
    if count > FEW_ROWS:
        done = by_high + by_low
        return done[:count] + done[count:]
    return by_high[:count] + (by_high[count:] + by_low)


def split(pieces, places, high_ref, low_ref, before=0):
    for piece in pieces:
        lines, slots, panel_rows, _ = piece.shape

        def body(j, carry, before=before, piece=piece):
            rows = pl.ds(pl.multiple_of(places[before + j] * panel_rows, panel_rows), panel_rows)
            for slot in range(slots):
                high, low = halves(piece[j, slot])
                high_ref[slot, rows, :] = high
                low_ref[slot, rows, :] = low
            return carry

        lax.fori_loop(0, lines, body, 0)
        before += lines


def layer_kernel(*refs):
    pieces, refs = refs[:PIECES], refs[PIECES:]
    wave_decay, places, facts, thickness, refl_out, trans_out, decays_out = refs[:7]
    high_out, low_out, high, low, decay_row, sem, sems = refs[7:]
    copy = pltpu.make_async_copy(wave_decay.at[pl.ds(facts[1], 1)], decay_row, sem)
    copy.start()
    split(pieces, places, high, low)
    saves = [pltpu.make_async_copy(high, high_out, sems.at[0]), pltpu.make_async_copy(low, low_out, sems.at[1])]
    for save in saves:
        save.start()
    copy.wait()
    rows, order = pieces[0].shape[2:]
    decays = jnp.exp(-decay_row[...] * thickness[0])
    decays_out[...] = decays
    row_ids = facts[0] + lax.broadcasted_iota(jnp.int32, (rows, order), 0)
    eye = row_ids == lax.broadcasted_iota(jnp.int32, (rows, order), 1)
    own_decays = jnp.sum(jnp.where(eye, decays, 0.0), axis=1, keepdims=True)
    term = product(own_decays * pieces[0][0, 0] * decays, high.at[0], low.at[0])

    def body(k, carry):
        term, summed = carry
        term = product(term * decays, high.at[0], low.at[0])
        term = product(term * decays, high.at[0], low.at[0])
        return term, summed + term

    _, summed = lax.fori_loop(0, TERMS - 2, body, (term, jnp.where(eye, 1.0, 0.0) + term))
    scaled = summed * decays
    both = product(jnp.concatenate([scaled, summed], axis=0), high.at[0], low.at[0])
    refl_out[...] = both[:rows] * decays - both[rows:]
    trans_out[...] = scaled - product(both[:rows], high.at[0], low.at[0])
    for save in saves:
        save.wait()


def pair_kernel(*refs):
    own_pieces, oth_pieces, refs = refs[: PIECES - 1], refs[PIECES - 1 : 2 * PIECES - 2], refs[2 * PIECES - 2 :]
    high_in, low_in, own_far, oth_far, places, inner, own_refl, own_trans, oth_trans, decay_row = refs[:10]
    refl_out, trans_out, far_out, own_high, own_low, oth_high, oth_low, layer_high, layer_low, stage, sems = refs[10:]
    brought = [
        pltpu.make_async_copy(own_far, stage.at[0], sems.at[2]),
        pltpu.make_async_copy(oth_far, stage.at[1], sems.at[3]),
    ]
    for load in brought:
        load.start()
    loads = [
        pltpu.make_async_copy(high_in, layer_high, sems.at[0]),
        pltpu.make_async_copy(low_in, layer_low, sems.at[1]),
    ]
    for load in loads:
        load.start()
    split(own_pieces, places, own_high, own_low)
    split(oth_pieces[:SIDE], places, oth_high, oth_low)
    split(oth_pieces[SIDE:], places, oth_high, oth_low, before=(SIDE + 1) * SIDE)
    for load in brought:
        load.wait()
    split([stage.at[0]], places, own_high, own_low, before=(PIECES - 1) * SIDE)
    split([stage.at[1]], places, oth_high, oth_low, before=SIDE * SIDE)
    first = product(own_trans[...], oth_high.at[0], oth_low.at[0])
    both = jnp.concatenate([first, oth_trans[...]], axis=0)

    def chain(k, carry):
        both, summed = carry
        both = product(both, own_high.at[0], own_low.at[0])
        both = product(both, oth_high.at[0], oth_low.at[0])
        return both, summed + both

    _, summed = lax.fori_loop(0, TERMS - 1, chain, (both, both))
    decays = decay_row[...]
    for load in loads:
        load.wait()

    def layer(rows):
        return product(rows, layer_high.at[0], layer_low.at[0])

    def series(k, carry):
        term, summed = carry
        term = layer(layer(term * decays) * decays)
        return term, summed + term

    _, summed = lax.fori_loop(0, TERMS - 1, series, (summed, summed))
    scaled = summed * decays
    done = scaled - layer(layer(scaled))
    rows = own_refl.shape[0]
    refl, trans = own_refl[...] + done[:rows], done[rows:]
    refl_out[...] = refl
    trans_out[...] = trans
    far_out[...] = jnp.where(inner[0] == 1, refl, trans)


def last_chain(*refs):
    pieces, refs = refs[:PIECES], refs[PIECES:]
    places, inner, own_trans, near_trans, out, high, low = refs
    split(pieces, places, high, low)
    first, second = 1 - inner[0], inner[0]
    term = jnp.where(inner[0] == 1, own_trans[...], near_trans[...])
    half = product(term, high.at[first], low.at[first])

    def body(k, carry):
        half, term_sum, half_sum = carry
        term = product(half, high.at[second], low.at[second])
        half = product(term, high.at[first], low.at[first])
        return half, term_sum + term, half_sum + half

    _, term_sum, half_sum = lax.fori_loop(0, TERMS - 1, body, (half, term, half))
    out[...] = jnp.where(inner[0] == 1, term_sum, half_sum)


def last_close(*refs):
    pieces, refs = refs[:SIDE], refs[SIDE:]
    places, summed, oth_summed, own_out, oth_out, high, low = refs
    split(pieces, places, high, low)
    rows, order = summed.shape
    empty = jnp.zeros((rows, order), jnp.bfloat16)

    def clear(j, carry):
        part = pl.ds(pl.multiple_of(places[SIDE * SIDE + j] * rows, rows), rows)
        high[0, part, :] = empty
        low[0, part, :] = empty
        return carry

    lax.fori_loop(0, SIDE * SIDE, clear, 0)
    both = jnp.concatenate([summed[...], oth_summed[...]], axis=0)
    done = product(both, high.at[0], low.at[0])
    own_out[...] = done[:rows]
    oth_out[...] = done[rows:]


def call(kernel, room, steps, outs, pieces, tables, small, far=(), scratch=(), placed=True):
    vmem = pl.BlockSpec(memory_space=pltpu.VMEM)
    here = [pltpu.with_memory_space_constraint(a, pltpu.VMEM) for a in (*pieces, *small)]
    far = [pltpu.with_memory_space_constraint(a, pltpu.HBM) for a in far]
    used = sum(math.prod(a.shape) * 2 for a in scratch if len(a.shape) == 3)
    return pl.pallas_call(
        kernel,
        out_shape=tuple(
            out if placed else jax.ShapeDtypeStruct(out.shape, out.dtype) for out in outs
        ),
        in_specs=[vmem] * len(pieces)
        + [pl.BlockSpec(memory_space=pl.ANY)] * len(far)
        + [pl.BlockSpec(memory_space=pltpu.SMEM)] * len(tables)
        + [vmem] * len(small),
        out_specs=tuple(vmem if out.dtype == jnp.float32 else pl.BlockSpec(memory_space=pl.ANY) for out in outs),
        scratch_shapes=list(scratch),
        cost_estimate=pl.CostEstimate(
            flops=steps * 6 * 64 * 1024 * 1024, transcendentals=0, bytes_accessed=steps * MATRIX_BYTES
        ),
        compiler_params=pltpu.CompilerParams(vmem_limit_bytes=used + room * 1024 * 1024),
    )(*here[: len(pieces)], *far, *tables, *here[len(pieces) :])


def matrices(slots, order, space=pltpu.VMEM):
    return (space((slots, order, order), jnp.bfloat16),) * 2


def panel_of(x, y, core):
    return (x % SIDE * SIDE + y % SIDE) * 2 + core


def moved(block, phase, step):
    route = []
    for x in range(SIDE):
        for y in range(SIDE):
            for core in range(2):
                along_x = core == phase
                target = panel_of(x + step, y, core) if along_x else panel_of(x, y + step, core)
                route.append((panel_of(x, y, core), target))
    return lax.ppermute(block, "panel", route)


def line_of(rows):
    return [rows] + [moved(rows, 0, step) for step in STEPS]


def spread(line):
    return [line] + [moved(line, 1, step) for step in STEPS]


def other_core(block):
    return lax.ppermute(block, "panel", [(i, i ^ 1) for i in range(2 * SIDE * SIDE)])


def flipped(pieces):
    return pieces + [other_core(piece) for piece in pieces]


def places_of(panel):
    x, y, core = panel // (2 * SIDE), panel // 2 % SIDE, panel % 2
    back = jnp.array((0,) + STEPS, jnp.int32)
    found = []
    for owner in (core, 1 - core):
        outer, inner = back[:, None], back[None, :]
        along_x = panel_of(x - inner + SIDE, y - outer + SIDE, 0)
        along_y = panel_of(x - outer + SIDE, y - inner + SIDE, 1)
        found.append(jnp.where(owner == 0, along_x, along_y).reshape(-1))
    return jnp.concatenate(found)


def local(reflections, wave_decay, thickness, material):
    panel_rows = reflections.shape[1]
    order = reflections.shape[2]
    rows = (panel_rows, order)
    panel = lax.axis_index("panel")
    layer = lax.axis_index("layer")
    places = places_of(panel)
    inner = (layer == 1) | (layer == 2)
    inner_flag = inner.astype(jnp.int32)[None]
    facts = jnp.stack([panel * panel_rows, material[0]])
    own = lax.dynamic_index_in_dim(reflections, material[0], 0, keepdims=False)
    own, places, facts = lax.optimization_barrier((own, places, facts))
    block = pltpu.VMEM(rows, jnp.float32)
    refl, trans, decays, *halved = call(
        layer_kernel, 10, 2 * TERMS, (block, block, pltpu.VMEM((1, order), jnp.float32), *matrices(1, order, pltpu.HBM)),
        flipped(spread(jnp.stack(line_of(own[None])))), (places, facts, thickness), (), far=(wave_decay,),
        scratch=(
            *matrices(1, order), pltpu.VMEM((1, order), jnp.float32),
            pltpu.SemaphoreType.DMA(()), pltpu.SemaphoreType.DMA((2,)),
        ),
    )
    pairs = [(0, 1), (1, 0), (2, 3), (3, 2)]
    line = jnp.stack(line_of(refl[None]))
    oth_line = lax.ppermute(line, "layer", pairs)
    oth_trans = lax.ppermute(trans, "layer", pairs)
    mine = spread(line)
    oth_line, oth_trans, mine[3] = lax.optimization_barrier((oth_line, oth_trans, mine[3]))
    own_pieces, oth_pieces = flipped(mine), flipped(spread(oth_line))
    refl, trans, away = call(
        pair_kernel, 16, 4 * TERMS, (block, block, block),
        own_pieces[: PIECES - 1] + oth_pieces[:SIDE] + oth_pieces[SIDE + 1 :], (places, inner_flag),
        (refl, trans, oth_trans, decays), far=(*halved, own_pieces[PIECES - 1], oth_pieces[SIDE]),
        scratch=matrices(1, order) * 3
        + (pltpu.VMEM((2, SIDE, 1, *rows), jnp.float32), pltpu.SemaphoreType.DMA((4,))),
    )
    far = lax.ppermute(away, "layer", [(0, 2), (2, 0), (1, 3), (3, 1)])
    near = lax.ppermute(refl, "layer", [(1, 0), (2, 3)])
    cross = lax.ppermute(refl, "layer", [(1, 2), (2, 1)])
    blocks = jnp.stack(
        [jnp.where(inner, cross, near), jnp.where(inner, refl, far), jnp.where(inner, far, trans)]
    )
    near_trans = lax.ppermute(trans, "layer", [(1, 0), (2, 3)])
    line = line_of(blocks)
    mine = spread(jnp.stack([part[:2] for part in line]))
    rest = jnp.stack([part[2:] for part in line])
    rest, *_ = lax.optimization_barrier((rest, *mine[1:]))
    rest = spread(rest)
    (summed,) = call(
        last_chain, 12, 2 * TERMS, (block,), flipped(mine), (places, inner_flag), (trans, near_trans), scratch=matrices(2, order)
    )
    *rest, summed = lax.optimization_barrier((*rest, summed))
    own_part, oth_part = call(
        last_close, 10, 2, (block, block), rest, (places,), (summed, other_core(summed)), scratch=matrices(1, order)
    )
    out = jnp.where(inner, 0.0, refl) + (own_part + other_core(oth_part))
    return out[None]


def solution(mesh):
    placed = (P(None, "panel", None), P(), P("layer"), P("layer"))
    return jax.shard_map(
        local, mesh=mesh, in_specs=placed, out_specs=P("layer", "panel", None), check_vma=False
    )
```
